32 devices in a mesh: row: 4 (over x, core), col: 8 (over z, y).
Axes of the slice: x: 2, y: 2, z: 4, core: 2. Of those that a mesh axis runs over, the one named last changes fastest.
Arguments:
- object_field: float32 [2, 2048, 4096], P(None, 'row', 'col'), may hold values from -6 to 6
- probe: float32 [2, 256, 256], replicated, may hold values from -6 to 6
- dual: float32 [2, 4, 8, 4, 256, 256], P(None, 'row', 'col'), may hold values from -4 to 4
- amplitude: float32 [4, 8, 4, 256, 256], P('row', 'col'), may hold values from 0.1 to 3
- offsets: int32 [2, 4, 8, 4], P(None, 'row', 'col'), may hold values from 0 to 511
- live: int32 [4, 8], P('row', 'col'), may hold values from 1 to 4, as said below
Outputs:
- object_new: float32 [2, 2048, 4096], P(None, 'row', 'col')
- dual_new: float32 [2, 4, 8, 4, 256, 256], P(None, 'row', 'col')
The draws below stay inside these ranges and needn't reach their ends.
Inputs may be any that keep to these rules, and one draw needn't show every extreme that they name: `offsets`: each slot's probe centre lies inside its own tile. `live`: the used slots of a tile are its first ones; some tile uses all 4 slots.
All inputs are finite; a program needn't handle non-finite values.
Results may differ from the reference program's by a relative error of at most 0.00022.
Values sent between devices are 32-bit elements; how exact they have to be, the bound alone decides.
A program may use at most 128 MiB of HBM per device.

```python
import math
import jax
import jax.numpy as jnp
from jax import lax

PS = 256
TILE = 512
NP = 4
GRID_R = 4
GRID_C = 8
NR = 2048
NC = 4096


def draw_live(key, part):
    first, second = jax.random.split(jax.random.fold_in(key, 7))
    counts = jax.random.randint(first, (GRID_R * GRID_C,), 1, NP + 1)
    chosen = jax.random.randint(second, (), 0, GRID_R * GRID_C)
    counts = jnp.where(jnp.arange(GRID_R * GRID_C) == chosen, NP, counts)
    return counts.reshape(GRID_R, GRID_C).astype(jnp.int32)


def with_ends(result, own_key, least, high):
    shape = result.shape
    spot = [jax.random.randint(jax.random.fold_in(own_key, axis), (), 0, shape[axis]) for axis in range(len(shape))]
    result = result.at[tuple(spot)].set(least)
    longest = shape.index(max(shape))
    spot[longest] = (spot[longest] + 1) % shape[longest]
    return result.at[tuple(spot)].set(high)


def steps_of(rng, shape, cuts, smallest, high):
    loudness, own = 1.0, jax.random.fold_in(rng, 6)
    for axis_at, blocks in cuts:
        heights = jnp.exp(jax.random.uniform(jax.random.fold_in(own, axis_at), (blocks,), jnp.float32, smallest / len(cuts), high / len(cuts)))
        loudness = loudness * jnp.repeat(heights, shape[axis_at] // blocks).reshape([-1 if axis == axis_at else 1 for axis in range(len(shape))])
    return loudness


def bell_draw(key, extent, spread, limit, cuts=(), kind=jnp.bfloat16):
    factor_of = steps_of(key, extent, cuts, -0.22, 0.18) if cuts else 1.0
    drawn = jax.random.normal(key, extent, jnp.float32) * spread * factor_of
    return jnp.minimum(jnp.maximum(drawn, -limit), limit).astype(kind)


def setup_inputs(seed: int = 0) -> dict:
    keys = jax.random.split(jax.random.key(seed), 7)
    return {
        "object_field": bell_draw(keys[0], (2, NR, NC), 1.0, 6.0, ((1, 4), (2, 8)), jnp.float32),
        "probe": bell_draw(keys[1], (2, PS, PS), 1.0, 6.0, (), jnp.float32),
        "dual": bell_draw(keys[2], (2, GRID_R, GRID_C, NP, PS, PS), 0.5, 4.0, ((1, 4), (2, 8)), jnp.float32),
        "amplitude": jnp.clip(jnp.exp(math.log(3.0) - 3.4011974 * jax.random.uniform(keys[3], (GRID_R, GRID_C, NP, PS, PS), jnp.float32) ** steps_of(keys[3], (GRID_R, GRID_C, NP, PS, PS), ((0, 4), (1, 8)), -0.2, 0.2)), 0.1, 3.0),
        "offsets": with_ends(jax.random.randint(keys[4], (2, GRID_R, GRID_C, NP), 0, TILE), jax.random.fold_in(keys[4], 1), 0, TILE - 1).astype(jnp.int32),
        "live": draw_live(jax.random.fold_in(keys[6], 71), 0),
    }


FLOOR = 0.1
BETA = 1.0


def reference(object_field, probe, dual, amplitude, offsets, live):
    half = PS // 2
    count = GRID_R * GRID_C * NP
    probe_c = probe[0] + 1j * probe[1]
    power = probe[0] * probe[0] + probe[1] * probe[1]
    padded = jnp.pad(object_field, ((0, 0), (half, half), (half, half)))
    tops = ((jnp.arange(GRID_R) * TILE)[:, None, None] + offsets[0]).astype(jnp.int32).reshape(count)
    lefts = ((jnp.arange(GRID_C) * TILE)[None, :, None] + offsets[1]).astype(jnp.int32).reshape(count)
    used = (jnp.arange(NP)[None, None, :] < live[:, :, None]).astype(object_field.dtype).reshape(count)
    duals = jnp.moveaxis(dual, 0, 3).reshape(count, 2, PS, PS)
    amps = amplitude.reshape(count, PS, PS)
    zero = jnp.int32(0)

    def forward(acc, item):
        top, left, lam, amp, use = item
        patch = lax.dynamic_slice(padded, (zero, top, left), (2, PS, PS))
        lam_c = lam[0] + 1j * lam[1]
        wave = probe_c * (patch[0] + 1j * patch[1]) + lam_c
        spec = jnp.fft.fft2(wave, norm="ortho")
        spec = amp * spec / jnp.maximum(jnp.abs(spec), FLOOR)
        exit_wave = jnp.fft.ifft2(spec, norm="ortho")
        diff = jnp.conj(probe_c) * (exit_wave - lam_c)
        piece = use * jnp.stack((diff.real, diff.imag, power))
        current = lax.dynamic_slice(acc, (zero, top, left), (3, PS, PS))
        acc = lax.dynamic_update_slice(acc, current + piece, (zero, top, left))
        return acc, jnp.stack((exit_wave.real, exit_wave.imag))

    start = jnp.zeros((3, GRID_R * TILE + PS, GRID_C * TILE + PS), object_field.dtype)
    acc, exits = lax.scan(forward, start, (tops, lefts, duals, amps, used))
    sums = acc[:, half:half + GRID_R * TILE, half:half + GRID_C * TILE]
    object_new = (sums[:2] + BETA * object_field) / (sums[2] + BETA)
    padded_new = jnp.pad(object_new, ((0, 0), (half, half), (half, half)))

    def backward(item):
        top, left, lam, exit_wave, use = item
        patch = lax.dynamic_slice(padded_new, (zero, top, left), (2, PS, PS))
        lit = probe_c * (patch[0] + 1j * patch[1])
        return lam + use * (jnp.stack((lit.real, lit.imag)) - exit_wave)

    dual_new = lax.map(backward, (tops, lefts, duals, exits, used))
    dual_new = jnp.moveaxis(dual_new.reshape(GRID_R, GRID_C, NP, 2, PS, PS), 3, 0)
    return (object_new, dual_new)
```

```python
import functools
import math

import jax
import jax.numpy as jnp
import numpy as np
from jax import lax
from jax.experimental import pallas as pl
from jax.experimental.pallas import tpu as pltpu
from jax.sharding import PartitionSpec as P

FLOOR = 0.1
BETA = 1.0
LANES = 128
ROWS = 8
F32 = jnp.float32
BF16 = jnp.bfloat16
ANY = pl.BlockSpec(memory_space=pl.ANY)
VM = pl.BlockSpec(memory_space=pltpu.VMEM)
SM = pl.BlockSpec(memory_space=pltpu.SMEM)


def shift(value, axis, by):
    count = lax.axis_size(axis)
    pairs = [(i, i + by) for i in range(count) if 0 <= i + by < count]
    return lax.ppermute(value, axis, pairs)


def tables(size):
    n = size // 2
    k = np.arange(n)
    angle = 2.0 * math.pi * ((k[:, None] * k[None, :]) % n) / n
    c, s = np.cos(angle) / math.sqrt(size), np.sin(angle) / math.sqrt(size)
    fwd = np.block([[c, s], [-s, c]])
    inv = np.block([[c, -s], [s, c]])
    parts = []
    for full in (fwd, inv):
        hi = full.astype(np.float32).astype(BF16)
        parts += [hi, (full - hi.astype(np.float64)).astype(np.float32).astype(BF16)]
    perm = np.zeros((size, size), np.float32)
    perm[2 * k, k] = 1.0
    perm[2 * k + 1, n + k] = 1.0
    tw = 2.0 * math.pi * k / size
    ct, st = np.cos(tw).astype(np.float32), np.sin(tw).astype(np.float32)
    rows = np.stack([np.broadcast_to(ct[:, None], (n, size)), np.broadcast_to(st[:, None], (n, size))])
    cols = np.stack([np.broadcast_to(ct[None, :], (size, n)), np.broadcast_to(st[None, :], (size, n))])
    return [jnp.asarray(np.stack(parts)), jnp.asarray(perm.astype(BF16)), jnp.asarray(rows), jnp.asarray(cols)]


def split(x):
    hi = x.astype(BF16)
    return hi, (x - hi.astype(F32)).astype(BF16)


def dot(a, b):
    return jnp.dot(a, b, preferred_element_type=F32)


def left_dot(wh, wl, x):
    xh, xl = split(x)
    return dot(wl, xh) + dot(wh, xl) + dot(wh, xh)


def right_dot(x, wh, wl):
    xh, xl = split(x)
    return dot(xh, wl) + dot(xl, wh) + dot(xh, wh)


def cat(parts, axis):
    return jnp.concatenate(parts, axis=axis)


def load_window(ext, channel, top, left, size):
    row = pl.multiple_of((top // ROWS) * ROWS, ROWS)
    base = pl.multiple_of((left // LANES) * LANES, LANES)
    width, height = size + LANES, size + ROWS
    wide = ext[channel, pl.ds(row, height), pl.ds(base, width)]
    wide = pltpu.roll(wide, (width - (left - base)) % width, 1)[:, :size]
    return pltpu.roll(wide, (height - (top - row)) % height, 0)[:size]


def add_window(acc, channel, top, left, value):
    size = value.shape[0]
    row = pl.multiple_of((top // ROWS) * ROWS, ROWS)
    base = pl.multiple_of((left // LANES) * LANES, LANES)
    width, height = size + LANES, size + ROWS
    wide = cat([value, jnp.zeros((ROWS, size), F32)], 0)
    wide = pltpu.roll(wide, top - row, 0)
    wide = cat([wide, jnp.zeros((height, LANES), F32)], 1)
    wide = pltpu.roll(wide, left - base, 1)
    acc[channel, pl.ds(row, height), pl.ds(base, width)] += wide


def halo_copies(tile, half, refs, ext, sems):
    cells, up, down, lm, le, rm, re, cu, cd = refs
    end, far = half + tile, half + tile
    mid = tile - 2 * half
    jobs = [
        (cells, ext.at[:, half:end, half:end]),
        (up, ext.at[:, :half, half:end]),
        (down, ext.at[:, far:, half:end]),
        (lm, ext.at[:, 2 * half : 2 * half + mid, :half]),
        (rm, ext.at[:, 2 * half : 2 * half + mid, far:]),
        (le.at[:, 0], ext.at[:, half : 2 * half, :half]),
        (le.at[:, 1], ext.at[:, tile:end, :half]),
        (re.at[:, 0], ext.at[:, half : 2 * half, far:]),
        (re.at[:, 1], ext.at[:, tile:end, far:]),
        (cu.at[:, 0], ext.at[:, :half, :half]),
        (cu.at[:, 1], ext.at[:, :half, far:]),
        (cd.at[:, 0], ext.at[:, far:, :half]),
        (cd.at[:, 1], ext.at[:, far:, far:]),
    ]
    return [pltpu.make_async_copy(a, b, sems.at[i]) for i, (a, b) in enumerate(jobs)]


N_HALO = 13


def project_kernel(tile, half, info, *refs):
    halo, rest = refs[:9], refs[9:]
    probe, dual, amp, wt, perm, twr, twc = rest[:7]
    base, o_up, o_dn, o_c, o_lm, o_le, o_rm, o_re = rest[7:15]
    ext, acc, strips, sems, osems = rest[15:]
    slot = pl.program_id(0)
    slots = pl.num_programs(0)
    size = 2 * half

    @pl.when(slot == 0)
    def _():
        copies = halo_copies(tile, half, halo, ext, sems)
        for c in copies:
            c.start()
        acc[...] = jnp.zeros_like(acc)
        for c in copies:
            c.wait()

    active = slot < info[2 * slots]

    @pl.when(jnp.logical_not(active))
    def _():
        base[...] = dual[...]

    @pl.when(active)
    def _():
        top = info[slot]
        left = info[slots + slot]
        pr, pi = probe[0], probe[1]
        sr = load_window(ext, 0, top, left, size)
        si = load_window(ext, 1, top, left, size)
        re = pr * sr - pi * si + dual[0, 0]
        im = pr * si + pi * sr + dual[1, 0]
        fh, fl, ih, il = wt[0], wt[1], wt[2], wt[3]
        cr, sr_ = twr[0], twr[1]
        cc, sc = twc[0], twc[1]
        dr, di = re[:half] - re[half:], im[:half] - im[half:]
        x = cat(
            [
                cat([re[:half] + re[half:], dr * cr + di * sr_], 1),
                cat([im[:half] + im[half:], di * cr - dr * sr_], 1),
            ],
            0,
        )
        y = left_dot(fh, fl, x)
        re = cat([y[:half, :size], y[:half, size:]], 0)
        im = cat([y[half:, :size], y[half:, size:]], 0)
        dr, di = re[:, :half] - re[:, half:], im[:, :half] - im[:, half:]
        x = cat(
            [
                cat([re[:, :half] + re[:, half:], im[:, :half] + im[:, half:]], 1),
                cat([dr * cc + di * sc, di * cc - dr * sc], 1),
            ],
            0,
        )
        s = right_dot(x, ih, il)
        for c in range(size // LANES):
            strips[c] = amp[0, :, c * LANES : (c + 1) * LANES]
        a = cat(
            [
                cat([strips[c, pl.ds(first, half, stride=2), :] for c in range(size // LANES)], 1)
                for first in range(2)
            ],
            0,
        )
        ah, al = split(a)
        a = dot(ah, perm[...]) + dot(al, perm[...])
        a = cat([a[:, :half], a[:, half:]], 0)
        sre, sim = s[:, :half], s[:, half:]
        fac = a * lax.rsqrt(jnp.maximum(sre * sre + sim * sim, FLOOR * FLOOR))
        x = cat([sre * fac, sim * fac], 1)
        z = right_dot(x, fh, fl)
        er, ei = z[:size, :half], z[:size, half:]
        orr, oi = z[size:, :half], z[size:, half:]
        tr, ti = orr * cc - oi * sc, oi * cc + orr * sc
        re = cat([er + tr, er - tr], 1)
        im = cat([ei + ti, ei - ti], 1)
        x = cat([cat([re[:half], re[half:]], 1), cat([im[:half], im[half:]], 1)], 0)
        y = left_dot(ih, il, x)
        er, ei = y[:half, :size], y[half:, :size]
        orr, oi = y[:half, size:], y[half:, size:]
        tr, ti = orr * cr - oi * sr_, oi * cr + orr * sr_
        dr = cat([er + tr, er - tr], 0) - dual[0, 0]
        di = cat([ei + ti, ei - ti], 0) - dual[1, 0]
        base[0, 0] = -dr
        base[1, 0] = -di
        add_window(acc, 0, top, left, pr * dr + pi * di)
        add_window(acc, 1, top, left, pr * di - pi * dr)

    @pl.when(slot == slots - 1)
    def _():
        end = half + tile
        jobs = [
            (acc.at[:, :half, :], o_up),
            (acc.at[:, end:, :], o_dn),
            (acc.at[:, size:tile, :half], o_lm),
            (acc.at[:, size:tile, end:], o_rm),
            (acc.at[:, half:size, :half], o_le.at[:, 0]),
            (acc.at[:, tile:end, :half], o_le.at[:, 1]),
            (acc.at[:, half:size, end:], o_re.at[:, 0]),
            (acc.at[:, tile:end, end:], o_re.at[:, 1]),
            (acc.at[:, half:end, half:end], o_c),
        ]
        copies = [pltpu.make_async_copy(a, b, osems.at[i]) for i, (a, b) in enumerate(jobs)]
        for c in copies:
            c.start()
        for c in copies:
            c.wait()


def weight_kernel(tile, half, info, probe, out, acc, power):
    slots = (info.shape[0] // 9 - 1) // 2
    size = 2 * half
    acc[...] = jnp.zeros_like(acc)
    power[...] = probe[0] * probe[0] + probe[1] * probe[1]

    def body(index, carry):
        owner = index // slots
        slot = index % slots
        at = owner * (2 * slots + 1)
        top = info[at + slot] + (owner // 3 - 1) * tile + half
        left = info[at + slots + slot] + (owner % 3 - 1) * tile + half
        live = info[at + 2 * slots]
        hit = (slot < live) & (top > 0) & (top < size + tile) & (left > 0) & (left < size + tile)

        @pl.when(hit)
        def _():
            add_window(acc, 0, top, left, power[...])

        return carry

    lax.fori_loop(0, 9 * slots, body, 0)
    out[...] = acc[0, size : size + tile, size : size + tile] + BETA


def update_kernel(tile, half, cells, sums, weight, fa, fb, lm, le, rm, re, out, o_lm, o_le, o_rm, o_re):
    size = 2 * half
    end = half + tile
    mid = slice(size - half, tile - half)
    inv = 1.0 / weight[...]
    for ch in range(2):
        total = sums[ch] + BETA * cells[ch]
        topped = total[:half] + fa[ch, :, half:end]
        bottom = total[tile - half :] + fb[ch, :, half:end]
        total = cat([topped, total[mid], bottom], 0)
        from_left = cat([le[ch, 0], lm[ch], le[ch, 1]], 0)
        from_right = cat([re[ch, 0], rm[ch], re[ch, 1]], 0)
        head = total[:, :half] + from_left
        tail = total[:, tile - half :] + from_right
        new = cat([head, total[:, half : tile - half], tail], 1) * inv
        out[ch] = new
        o_lm[ch] = new[mid, :half]
        o_rm[ch] = new[mid, tile - half :]
        for i, rows in enumerate((slice(0, half), slice(tile - half, tile))):
            o_le[ch, i] = new[rows, :half]
            o_re[ch, i] = new[rows, tile - half :]


def dual_kernel(tile, half, info, *refs):
    halo, rest = refs[:9], refs[9:]
    probe, base, out, ext, sems = rest
    slot = pl.program_id(0)
    slots = pl.num_programs(0)
    size = 2 * half

    @pl.when(slot == 0)
    def _():
        copies = halo_copies(tile, half, halo, ext, sems)
        for c in copies:
            c.start()
        for c in copies:
            c.wait()

    active = slot < info[2 * slots]

    @pl.when(jnp.logical_not(active))
    def _():
        out[...] = base[...]

    @pl.when(active)
    def _():
        top = info[slot]
        left = info[slots + slot]
        pr, pi = probe[0], probe[1]
        sr = load_window(ext, 0, top, left, size)
        si = load_window(ext, 1, top, left, size)
        out[0, 0] = base[0, 0] + (pr * sr - pi * si)
        out[1, 0] = base[1, 0] + (pr * si + pi * sr)


def halo(cells, pieces, half):
    lm, le, rm, re = pieces
    tile = cells.shape[1]
    got_le = shift(re, "col", 1)
    got_re = shift(le, "col", -1)
    up = shift(cells[:, tile - half :, :], "row", 1)
    down = shift(cells[:, :half, :], "row", -1)
    got_lm = shift(rm, "col", 1)
    got_rm = shift(lm, "col", -1)
    cu = shift(jnp.stack((got_le[:, 1], got_re[:, 1]), 1), "row", 1)
    cd = shift(jnp.stack((got_le[:, 0], got_re[:, 0]), 1), "row", -1)
    return cells, up, down, got_lm, got_le, got_rm, got_re, cu, cd


def shards(object_field, probe, dual, amplitude, offsets, live):
    tile = object_field.shape[1]
    size = probe.shape[1]
    half = size // 2
    slots = dual.shape[3]
    wide = tile + size
    mid = tile - size
    own = jnp.concatenate([offsets[0, 0, 0], offsets[1, 0, 0], live[0]])
    lam = dual.reshape(2, slots, size, size)
    amps = amplitude.reshape(slots, size, size)
    sd = lambda *shape: jax.ShapeDtypeStruct(shape, F32)

    band = jnp.stack([shift(own, "col", 1), own, shift(own, "col", -1)])
    around = jnp.concatenate([shift(band, "row", 1), band, shift(band, "row", -1)]).reshape(-1)

    head = object_field[:, :, :half]
    tail = object_field[:, :, tile - half :]
    ends = lambda x: jnp.stack((x[:, :half], x[:, tile - half :]), 1)
    inner = lambda x: x[:, half : tile - half]
    pieces = (inner(head), ends(head), inner(tail), ends(tail))
    around_cells = halo(object_field, pieces, half)

    weight = pl.pallas_call(
        functools.partial(weight_kernel, tile, half),
        out_shape=sd(tile, tile),
        in_specs=[SM, VM],
        out_specs=VM,
        scratch_shapes=[pltpu.VMEM((1, tile + 2 * size, tile + 2 * size), F32), pltpu.VMEM((size, size), F32)],
        cost_estimate=pl.CostEstimate(flops=20_000_000, bytes_accessed=8_000_000, transcendentals=0),
        name="weight",
    )(around, probe)

    slot_dual = pl.BlockSpec((2, 1, size, size), lambda j: (0, j, 0, 0))
    base, o_up, o_dn, o_c, o_lm, o_le, o_rm, o_re = pl.pallas_call(
        functools.partial(project_kernel, tile, half),
        grid=(slots,),
        out_shape=(
            sd(2, slots, size, size),
            sd(2, half, wide),
            sd(2, half, wide),
            sd(2, tile, tile),
            sd(2, mid, half),
            sd(2, 2, half, half),
            sd(2, mid, half),
            sd(2, 2, half, half),
        ),
        in_specs=[SM]
        + [ANY] * 9
        + [VM, slot_dual, pl.BlockSpec((1, size, size), lambda j: (j, 0, 0)), VM, VM, VM, VM],
        out_specs=(slot_dual,) + (ANY,) * 7,
        scratch_shapes=[
            pltpu.VMEM((2, wide, wide), F32),
            pltpu.VMEM((2, wide, wide), F32),
            pltpu.VMEM((size // LANES, size, LANES), F32),
            pltpu.SemaphoreType.DMA((N_HALO,)),
            pltpu.SemaphoreType.DMA((9,)),
        ],
        name="project",
    )(own, *around_cells, probe, lam, amps, *tables(size))

    got_rm = shift(o_lm, "col", -1)
    got_lm = shift(o_rm, "col", 1)
    fb = shift(o_up, "row", -1)
    fa = shift(o_dn, "row", 1)
    le = o_le + jnp.stack((fa[:, :, :half], fb[:, :, :half]), 1)
    re = o_re + jnp.stack((fa[:, :, tile + half :], fb[:, :, tile + half :]), 1)
    got_re = shift(le, "col", -1)
    got_le = shift(re, "col", 1)

    new, *new_pieces = pl.pallas_call(
        functools.partial(update_kernel, tile, half),
        out_shape=(sd(2, tile, tile), sd(2, mid, half), sd(2, 2, half, half), sd(2, mid, half), sd(2, 2, half, half)),
        in_specs=[VM] * 9,
        out_specs=(VM,) * 5,
        name="update",
    )(object_field, o_c, weight, fa, fb, got_lm, got_le, got_rm, got_re)

    around_new = halo(new, new_pieces, half)
    dual_new = pl.pallas_call(
        functools.partial(dual_kernel, tile, half),
        grid=(slots,),
        out_shape=sd(2, slots, size, size),
        in_specs=[SM] + [ANY] * 9 + [VM, slot_dual],
        out_specs=slot_dual,
        scratch_shapes=[pltpu.VMEM((2, wide, wide), F32), pltpu.SemaphoreType.DMA((N_HALO,))],
        name="renew",
    )(own, *around_new, probe, base)
    return new, dual_new.reshape(dual.shape)


def solution(mesh):
    placed = (
        P(None, "row", "col"),
        P(),
        P(None, "row", "col", None, None, None),
        P("row", "col", None, None, None),
        P(None, "row", "col", None),
        P("row", "col"),
    )
    return jax.shard_map(
        shards,
        mesh=mesh,
        in_specs=placed,
        out_specs=(P(None, "row", "col"), P(None, "row", "col", None, None, None)),
        check_vma=False,
    )
```

```python
import functools
import math

import jax
import jax.numpy as jnp
import numpy as np
from jax import lax
from jax.experimental import pallas as pl
from jax.experimental.pallas import tpu as pltpu
from jax.sharding import PartitionSpec as P

FLOOR = 0.1
BETA = 1.0
LANES = 128
ROWS = 8
SIDES = 16
F32 = jnp.float32
BF16 = jnp.bfloat16
ANY = pl.BlockSpec(memory_space=pl.ANY)
VM = pl.BlockSpec(memory_space=pltpu.VMEM)
SM = pl.BlockSpec(memory_space=pltpu.SMEM)


def tables(size):
    n = size // 2
    k = np.arange(n)
    angle = 2.0 * math.pi * ((k[:, None] * k[None, :]) % n) / n
    c, s = np.cos(angle) / math.sqrt(size), np.sin(angle) / math.sqrt(size)
    fwd = np.block([[c, s], [-s, c]])
    inv = np.block([[c, -s], [s, c]])
    parts = []
    for full in (fwd, inv):
        hi = full.astype(np.float32).astype(BF16)
        parts += [hi, (full - hi.astype(np.float64)).astype(np.float32).astype(BF16)]
    perm = np.zeros((size, size), np.float32)
    perm[2 * k, k] = 1.0
    perm[2 * k + 1, n + k] = 1.0
    tw = 2.0 * math.pi * k / size
    ct, st = np.cos(tw).astype(np.float32), np.sin(tw).astype(np.float32)
    rows = np.stack([np.broadcast_to(ct[:, None], (n, size)), np.broadcast_to(st[:, None], (n, size))])
    cols = np.stack([np.broadcast_to(ct[None, :], (size, n)), np.broadcast_to(st[None, :], (size, n))])
    return [jnp.asarray(np.stack(parts)), jnp.asarray(perm.astype(BF16)), jnp.asarray(rows), jnp.asarray(cols)]


def split(x):
    hi = x.astype(BF16)
    return hi, (x - hi.astype(F32)).astype(BF16)


def dot(a, b):
    return jnp.dot(a, b, preferred_element_type=F32)


def left_dot(wh, wl, x):
    xh, xl = split(x)
    return dot(wl, xh) + dot(wh, xl) + dot(wh, xh)


def right_dot(x, wh, wl):
    xh, xl = split(x)
    return dot(xh, wl) + dot(xl, wh) + dot(xh, wh)


def cat(parts, axis):
    return jnp.concatenate(parts, axis=axis)


def load_window(ext, channel, top, left, size):
    row = pl.multiple_of((top // ROWS) * ROWS, ROWS)
    base = pl.multiple_of((left // LANES) * LANES, LANES)
    width, height = size + LANES, size + ROWS
    wide = ext[channel, pl.ds(row, height), pl.ds(base, width)]
    wide = pltpu.roll(wide, (width - (left - base)) % width, 1)[:, :size]
    return pltpu.roll(wide, (height - (top - row)) % height, 0)[:size]


def add_window(acc, channel, top, left, value):
    size = value.shape[0]
    row = pl.multiple_of((top // ROWS) * ROWS, ROWS)
    base = pl.multiple_of((left // LANES) * LANES, LANES)
    width, height = size + LANES, size + ROWS
    wide = cat([value, jnp.zeros((ROWS, size), F32)], 0)
    wide = pltpu.roll(wide, top - row, 0)
    wide = cat([wide, jnp.zeros((height, LANES), F32)], 1)
    wide = pltpu.roll(wide, left - base, 1)
    acc[channel, pl.ds(row, height), pl.ds(base, width)] += wide


def load_halo(tile, half, info, cells, frame, ext, sems):
    end = half + tile
    jobs = [
        (frame.at[:, :half, :], ext.at[:, :half, :]),
        (frame.at[:, end:, :], ext.at[:, end:, :]),
        (frame.at[:, half:end, :half], ext.at[:, half:end, :half]),
        (frame.at[:, half:end, end:], ext.at[:, half:end, end:]),
        (cells, ext.at[:, half:end, half:end]),
    ]
    copies = [pltpu.make_async_copy(a, b, sems.at[i]) for i, (a, b) in enumerate(jobs)]
    for c in copies:
        c.start()

    def finish():
        for c in copies:
            c.wait()
        strips = (
            (slice(0, half), slice(None)),
            (slice(end, None), slice(None)),
            (slice(None), slice(0, half)),
            (slice(None), slice(end, None)),
        )
        for at, (rows, cols) in enumerate(strips):

            @pl.when(info[SIDES + at] == 0)
            def _():
                ext[:, rows, cols] = jnp.zeros_like(ext[:, rows, cols])

    return finish


class Grid:
    def __init__(self, send, recv):
        row, col = lax.axis_index("row"), lax.axis_index("col")
        self.has = {
            "up": row > 0,
            "down": row < lax.axis_size("row") - 1,
            "left": col > 0,
            "right": col < lax.axis_size("col") - 1,
        }
        self.peer = {"up": {"row": row - 1}, "down": {"row": row + 1}, "left": {"col": col - 1}, "right": {"col": col + 1}}
        self.back = {"up": "down", "down": "up", "left": "right", "right": "left"}
        self.send, self.recv = send, recv
        self.count = 0

    def greet(self):
        barrier = pltpu.get_barrier_semaphore()
        for side in self.has:

            @pl.when(self.has[side])
            def _():
                pl.semaphore_signal(barrier, inc=1, device_id=self.peer[side], device_id_type=pl.DeviceIdType.MESH)

        pl.semaphore_wait(barrier, sum(h.astype(jnp.int32) for h in self.has.values()))

    def message(self, side, src, dst, also=None):
        at = self.count
        self.count += 1
        copy = pltpu.make_async_remote_copy(
            src_ref=src,
            dst_ref=dst,
            send_sem=self.send.at[at],
            recv_sem=self.recv.at[at],
            device_id=self.peer[side],
            device_id_type=pl.DeviceIdType.MESH,
        )
        goes, comes = self.has[side], self.has[self.back[side]]
        if also is not None:
            goes, comes = goes & self.has[also], comes & self.has[also]
        return copy, goes, comes


def when(cond, act):
    if cond is True:
        act()
    else:
        pl.when(cond)(act)


def start(*messages):
    for copy, goes, _ in messages:
        pl.when(goes)(copy.start)


def arrive(*messages):
    for copy, _, comes in messages:
        pl.when(comes)(copy.wait_recv)


def leave(*messages):
    for copy, goes, _ in messages:
        pl.when(goes)(copy.wait_send)


def column_messages(grid, tile, half, src, frame):
    size, end = 2 * half, half + tile
    tops, bottoms, mids = slice(0, half), slice(tile - half, tile), slice(half, tile - half)
    ends, inner = [], []
    for rows, store, group in (
        (tops, slice(half, size), ends),
        (bottoms, slice(tile, end), ends),
        (mids, slice(size, tile), inner),
    ):
        group.append(grid.message("left", src.at[:, rows, :half], frame.at[:, store, end:]))
        group.append(grid.message("right", src.at[:, rows, tile - half :], frame.at[:, store, :half]))
    return ends, inner


def row_messages(grid, tile, half, src, frame):
    end = half + tile
    return [
        grid.message("up", src.at[:, :half, :], frame.at[:, end:, half:end]),
        grid.message("down", src.at[:, tile - half :, :], frame.at[:, :half, half:end]),
    ]


def corner_messages(grid, tile, half, frame):
    size, end = 2 * half, half + tile
    out = []
    for side, cols in (("left", slice(0, half)), ("right", slice(end, None))):
        out.append(grid.message("up", frame.at[:, half:size, cols], frame.at[:, end:, cols], also=side))
        out.append(grid.message("down", frame.at[:, tile:end, cols], frame.at[:, :half, cols], also=side))
    return out


def halo_kernel(tile, half, cells, info, frame, infos, send, recv, local):
    grid = Grid(send, recv)
    ends, inner = column_messages(grid, tile, half, cells, frame)
    rows = row_messages(grid, tile, half, cells, frame)
    corners = corner_messages(grid, tile, half, frame)
    tags = [
        grid.message("left", info.at[0], infos.at[1, 2]),
        grid.message("right", info.at[0], infos.at[1, 0]),
    ]
    bands = [
        grid.message("up", infos.at[1], infos.at[2]),
        grid.message("down", infos.at[1], infos.at[0]),
    ]
    fills = [
        (pltpu.make_async_copy(info.at[0], infos.at[1, 1], local.at[0]), True),
        (pltpu.make_async_copy(info.at[1], infos.at[1, 0], local.at[1]), jnp.logical_not(grid.has["left"])),
        (pltpu.make_async_copy(info.at[1], infos.at[1, 2], local.at[2]), jnp.logical_not(grid.has["right"])),
        (pltpu.make_async_copy(info.at[pl.ds(1, 3)], infos.at[0], local.at[3]), jnp.logical_not(grid.has["up"])),
        (pltpu.make_async_copy(info.at[pl.ds(1, 3)], infos.at[2], local.at[4]), jnp.logical_not(grid.has["down"])),
    ]
    for copy, cond in fills:
        when(cond, copy.start)
    grid.greet()
    start(*tags, *ends, *inner, *rows)
    for copy, cond in fills:
        when(cond, copy.wait)
    arrive(*tags)
    start(*bands)
    arrive(*ends)
    start(*corners)
    arrive(*inner, *rows, *bands, *corners)
    leave(*tags, *ends, *inner, *rows, *bands, *corners)


def update_kernel(tile, half, *refs):
    cells, sums, weight, p_le, p_re, o_up, o_dn, o_lm, o_rm = refs[:9]
    new, frame = refs[9:11]
    fa, fb, g_lm, g_rm, g_le, g_re, s_le, s_re, val, send, recv, local = refs[11:]
    size, end = 2 * half, half + tile
    grid = Grid(send, recv)
    has = grid.has
    up = grid.message("up", o_up, fb)
    down = grid.message("down", o_dn, fa)
    mids = [grid.message("left", o_lm, g_rm), grid.message("right", o_rm, g_lm)]
    ends = [grid.message("left", s_le, g_re), grid.message("right", s_re, g_le)]
    new_ends, new_inner = column_messages(grid, tile, half, val, frame)
    new_rows = row_messages(grid, tile, half, val, frame)
    corners = corner_messages(grid, tile, half, frame)
    grid.greet()
    start(up, down, *mids)
    for side, buffers in (("up", (fa,)), ("down", (fb,)), ("left", (g_lm, g_le)), ("right", (g_rm, g_re))):

        @pl.when(jnp.logical_not(has[side]))
        def _():
            for b in buffers:
                b[...] = jnp.zeros_like(b)

    arrive(up, down)
    for ch in range(2):
        s_le[ch, 0] = p_le[ch, 0] + fa[ch, :, :half]
        s_le[ch, 1] = p_le[ch, 1] + fb[ch, :, :half]
        s_re[ch, 0] = p_re[ch, 0] + fa[ch, :, end:]
        s_re[ch, 1] = p_re[ch, 1] + fb[ch, :, end:]
    start(*ends)
    tops, bottoms, inner = slice(0, half), slice(tile - half, tile), slice(half, tile - half)
    heads, tails = slice(0, half), slice(tile - half, tile)

    def settle(ch, rows, cols, more):
        total = sums[ch, rows, cols] + BETA * cells[ch, rows, cols]
        for m in more:
            total = total + m
        val[ch, rows, cols] = total / weight[rows, cols]

    for ch in range(2):
        settle(ch, inner, inner, ())
        settle(ch, tops, inner, (fa[ch, :, size:tile],))
        settle(ch, bottoms, inner, (fb[ch, :, size:tile],))
    arrive(*mids)
    for ch in range(2):
        settle(ch, inner, heads, (g_lm[ch],))
        settle(ch, inner, tails, (g_rm[ch],))
    start(*new_inner)
    arrive(*ends)
    for ch in range(2):
        settle(ch, tops, heads, (fa[ch, :, half:size], g_le[ch, 0]))
        settle(ch, bottoms, heads, (fb[ch, :, half:size], g_le[ch, 1]))
        settle(ch, tops, tails, (fa[ch, :, tile:end], g_re[ch, 0]))
        settle(ch, bottoms, tails, (fb[ch, :, tile:end], g_re[ch, 1]))
    start(*new_ends, *new_rows)
    keep = pltpu.make_async_copy(val, new, local.at[0])
    keep.start()
    arrive(*new_ends)
    start(*corners)
    arrive(*new_inner, *new_rows, *corners)
    keep.wait()
    leave(up, down, *mids, *ends, *new_ends, *new_inner, *new_rows, *corners)


def project_kernel(tile, half, info, *refs):
    halo, rest = refs[:2], refs[2:]
    probe, dual, amp, wt, perm, twr, twc = rest[:7]
    base, o_up, o_dn, o_c, o_lm, o_le, o_rm, o_re = rest[7:15]
    ext, acc, strips, sems, osems = rest[15:]
    slot = pl.program_id(0)
    slots = pl.num_programs(0)
    size = 2 * half

    @pl.when(slot == 0)
    def _():
        finish = load_halo(tile, half, info, *halo, ext, sems)
        acc[...] = jnp.zeros_like(acc)
        finish()

    active = slot < info[2 * slots]

    @pl.when(jnp.logical_not(active))
    def _():
        base[...] = dual[...]

    @pl.when(active)
    def _():
        top = info[slot]
        left = info[slots + slot]
        pr, pi = probe[0], probe[1]
        sr = load_window(ext, 0, top, left, size)
        si = load_window(ext, 1, top, left, size)
        re = pr * sr - pi * si + dual[0, 0]
        im = pr * si + pi * sr + dual[1, 0]
        fh, fl, ih, il = wt[0], wt[1], wt[2], wt[3]
        cr, sr_ = twr[0], twr[1]
        cc, sc = twc[0], twc[1]
        dr, di = re[:half] - re[half:], im[:half] - im[half:]
        x = cat(
            [
                cat([re[:half] + re[half:], dr * cr + di * sr_], 1),
                cat([im[:half] + im[half:], di * cr - dr * sr_], 1),
            ],
            0,
        )
        y = left_dot(fh, fl, x)
        re = cat([y[:half, :size], y[:half, size:]], 0)
        im = cat([y[half:, :size], y[half:, size:]], 0)
        dr, di = re[:, :half] - re[:, half:], im[:, :half] - im[:, half:]
        x = cat(
            [
                cat([re[:, :half] + re[:, half:], im[:, :half] + im[:, half:]], 1),
                cat([dr * cc + di * sc, di * cc - dr * sc], 1),
            ],
            0,
        )
        s = right_dot(x, ih, il)
        for c in range(size // LANES):
            strips[c] = amp[0, :, c * LANES : (c + 1) * LANES]
        a = cat(
            [
                cat([strips[c, pl.ds(first, half, stride=2), :] for c in range(size // LANES)], 1)
                for first in range(2)
            ],
            0,
        )
        ah, al = split(a)
        a = dot(ah, perm[...]) + dot(al, perm[...])
        a = cat([a[:, :half], a[:, half:]], 0)
        sre, sim = s[:, :half], s[:, half:]
        fac = a * lax.rsqrt(jnp.maximum(sre * sre + sim * sim, FLOOR * FLOOR))
        x = cat([sre * fac, sim * fac], 1)
        z = right_dot(x, fh, fl)
        er, ei = z[:size, :half], z[:size, half:]
        orr, oi = z[size:, :half], z[size:, half:]
        tr, ti = orr * cc - oi * sc, oi * cc + orr * sc
        re = cat([er + tr, er - tr], 1)
        im = cat([ei + ti, ei - ti], 1)
        x = cat([cat([re[:half], re[half:]], 1), cat([im[:half], im[half:]], 1)], 0)
        y = left_dot(ih, il, x)
        er, ei = y[:half, :size], y[half:, :size]
        orr, oi = y[:half, size:], y[half:, size:]
        tr, ti = orr * cr - oi * sr_, oi * cr + orr * sr_
        dr = cat([er + tr, er - tr], 0) - dual[0, 0]
        di = cat([ei + ti, ei - ti], 0) - dual[1, 0]
        base[0, 0] = -dr
        base[1, 0] = -di
        add_window(acc, 0, top, left, pr * dr + pi * di)
        add_window(acc, 1, top, left, pr * di - pi * dr)

    @pl.when(slot == slots - 1)
    def _():
        end = half + tile
        jobs = [
            (acc.at[:, :half, :], o_up),
            (acc.at[:, end:, :], o_dn),
            (acc.at[:, size:tile, :half], o_lm),
            (acc.at[:, size:tile, end:], o_rm),
            (acc.at[:, half:size, :half], o_le.at[:, 0]),
            (acc.at[:, tile:end, :half], o_le.at[:, 1]),
            (acc.at[:, half:size, end:], o_re.at[:, 0]),
            (acc.at[:, tile:end, end:], o_re.at[:, 1]),
            (acc.at[:, half:end, half:end], o_c),
        ]
        copies = [pltpu.make_async_copy(a, b, osems.at[i]) for i, (a, b) in enumerate(jobs)]
        for c in copies:
            c.start()
        for c in copies:
            c.wait()


def weight_kernel(tile, half, slots, info, probe, out, acc, power):
    size = 2 * half
    acc[...] = jnp.zeros_like(acc)
    power[...] = probe[0] * probe[0] + probe[1] * probe[1]

    def body(index, carry):
        owner = index // slots
        slot = index % slots
        r, c = owner // 3, owner % 3
        top = info[r, c, 0, slot] + (r - 1) * tile + half
        left = info[r, c, 0, slots + slot] + (c - 1) * tile + half
        live = info[r, c, 0, 2 * slots]
        hit = (slot < live) & (top > 0) & (top < size + tile) & (left > 0) & (left < size + tile)

        @pl.when(hit)
        def _():
            add_window(acc, 0, top, left, power[...])

        return carry

    lax.fori_loop(0, 9 * slots, body, 0)
    out[...] = acc[0, size : size + tile, size : size + tile] + BETA


def dual_kernel(tile, half, info, *refs):
    halo, rest = refs[:2], refs[2:]
    probe, base, out, new, ext, sems, keep_sem = rest
    keep = pltpu.make_async_copy(ext.at[:, half : half + tile, half : half + tile], new, keep_sem)
    slot = pl.program_id(0)
    slots = pl.num_programs(0)
    size = 2 * half

    @pl.when(slot == 0)
    def _():
        load_halo(tile, half, info, *halo, ext, sems)()
        keep.start()

    @pl.when(slot == slots - 1)
    def _():
        keep.wait()

    active = slot < info[2 * slots]

    @pl.when(jnp.logical_not(active))
    def _():
        out[...] = base[...]

    @pl.when(active)
    def _():
        top = info[slot]
        left = info[slots + slot]
        pr, pi = probe[0], probe[1]
        sr = load_window(ext, 0, top, left, size)
        si = load_window(ext, 1, top, left, size)
        out[0, 0] = base[0, 0] + (pr * sr - pi * si)
        out[1, 0] = base[1, 0] + (pr * si + pi * sr)


def shards(object_field, probe, dual, amplitude, offsets, live):
    tile = object_field.shape[1]
    size = probe.shape[1]
    half = size // 2
    slots = dual.shape[3]
    wide = tile + size
    mid = tile - size
    lam = dual.reshape(2, slots, size, size)
    amps = amplitude.reshape(slots, size, size)
    sd = lambda *shape: jax.ShapeDtypeStruct(shape, F32)
    dma = lambda n: pltpu.SemaphoreType.DMA((n,))

    row, col = lax.axis_index("row"), lax.axis_index("col")
    sides = [row > 0, row < lax.axis_size("row") - 1, col > 0, col < lax.axis_size("col") - 1]
    own = jnp.concatenate([offsets[0, 0, 0], offsets[1, 0, 0], live[0]])
    own = jnp.pad(own, (0, SIDES - own.shape[0]))
    own = jnp.concatenate([own, jnp.stack(sides).astype(jnp.int32)])
    tag = jnp.zeros((4, ROWS, LANES), jnp.int32).at[0, 0, : own.shape[0]].set(own)

    frame, infos = pl.pallas_call(
        functools.partial(halo_kernel, tile, half),
        out_shape=(sd(2, wide, wide), jax.ShapeDtypeStruct((3, 3, ROWS, LANES), jnp.int32)),
        in_specs=[ANY, ANY],
        out_specs=(ANY, ANY),
        scratch_shapes=[dma(16), dma(16), dma(5)],
        compiler_params=pltpu.CompilerParams(collective_id=0, has_side_effects=True),
        name="halo",
    )(object_field, tag)

    weight = pl.pallas_call(
        functools.partial(weight_kernel, tile, half, slots),
        out_shape=sd(tile, tile),
        in_specs=[SM, VM],
        out_specs=VM,
        scratch_shapes=[pltpu.VMEM((1, tile + 2 * size, tile + 2 * size), F32), pltpu.VMEM((size, size), F32)],
        name="weight",
    )(infos, probe)

    slot_dual = pl.BlockSpec((2, 1, size, size), lambda j: (0, j, 0, 0))
    base, o_up, o_dn, o_c, o_lm, o_le, o_rm, o_re = pl.pallas_call(
        functools.partial(project_kernel, tile, half),
        grid=(slots,),
        out_shape=(
            sd(2, slots, size, size),
            sd(2, half, wide),
            sd(2, half, wide),
            sd(2, tile, tile),
            sd(2, mid, half),
            sd(2, 2, half, half),
            sd(2, mid, half),
            sd(2, 2, half, half),
        ),
        in_specs=[SM, ANY, ANY, VM, slot_dual, pl.BlockSpec((1, size, size), lambda j: (j, 0, 0)), VM, VM, VM, VM],
        out_specs=(slot_dual,) + (ANY,) * 7,
        scratch_shapes=[
            pltpu.VMEM((2, wide, wide), F32),
            pltpu.VMEM((2, wide, wide), F32),
            pltpu.VMEM((size // LANES, size, LANES), F32),
            dma(5),
            dma(9),
        ],
        name="project",
    )(own, object_field, frame, probe, lam, amps, *tables(size))

    strip, side, end = (2, half, wide), (2, mid, half), (2, 2, half, half)
    new, frame = pl.pallas_call(
        functools.partial(update_kernel, tile, half),
        out_shape=(sd(2, tile, tile), sd(2, wide, wide)),
        in_specs=[VM] * 5 + [ANY] * 4,
        out_specs=(ANY, ANY),
        scratch_shapes=[pltpu.VMEM(x, F32) for x in (strip, strip, side, side, end, end, end, end, (2, tile, tile))]
        + [dma(18), dma(18), dma(1)],
        compiler_params=pltpu.CompilerParams(collective_id=1, has_side_effects=True),
        name="update",
    )(object_field, o_c, weight, o_le, o_re, o_up, o_dn, o_lm, o_rm)

    dual_new, new = pl.pallas_call(
        functools.partial(dual_kernel, tile, half),
        grid=(slots,),
        out_shape=(sd(2, slots, size, size), sd(2, tile, tile)),
        in_specs=[SM, ANY, ANY, VM, slot_dual],
        out_specs=(slot_dual, ANY),
        scratch_shapes=[pltpu.VMEM((2, wide, wide), F32), dma(5), pltpu.SemaphoreType.DMA],
        name="renew",
    )(own, new, frame, probe, base)
    return new, dual_new.reshape(dual.shape)


def solution(mesh):
    placed = (
        P(None, "row", "col"),
        P(),
        P(None, "row", "col", None, None, None),
        P("row", "col", None, None, None),
        P(None, "row", "col", None),
        P("row", "col"),
    )
    return jax.shard_map(
        shards,
        mesh=mesh,
        in_specs=placed,
        out_specs=(P(None, "row", "col"), P(None, "row", "col", None, None, None)),
        check_vma=False,
    )
```

```python
import functools
import math

import jax
import jax.numpy as jnp
import numpy as np
from jax import lax
from jax.experimental import pallas as pl
from jax.experimental.pallas import tpu as pltpu
from jax.sharding import PartitionSpec as P

FLOOR = 0.1
BETA = 1.0
LANES = 128
ROWS = 8
MIB = 1 << 20
F32 = jnp.float32
BF16 = jnp.bfloat16
ANY = pl.BlockSpec(memory_space=pl.ANY)
VM = pl.BlockSpec(memory_space=pltpu.VMEM)
SM = pl.BlockSpec(memory_space=pltpu.SMEM)


def tables(size):
    n = size // 2
    k = np.arange(n)
    angle = 2.0 * math.pi * ((k[:, None] * k[None, :]) % n) / n
    c, s = np.cos(angle) / math.sqrt(size), np.sin(angle) / math.sqrt(size)
    fwd = np.block([[c, s], [-s, c]])
    inv = np.block([[c, -s], [s, c]])
    parts = []
    for full in (fwd, inv):
        hi = full.astype(np.float32).astype(BF16)
        parts += [hi, (full - hi.astype(np.float64)).astype(np.float32).astype(BF16)]
    perm = np.zeros((size, size), np.float32)
    perm[2 * k, k] = 1.0
    perm[2 * k + 1, n + k] = 1.0
    tw = 2.0 * math.pi * k / size
    ct, st = np.cos(tw).astype(np.float32), np.sin(tw).astype(np.float32)
    rows = np.stack([np.broadcast_to(ct[:, None], (n, size)), np.broadcast_to(st[:, None], (n, size))])
    cols = np.stack([np.broadcast_to(ct[None, :], (size, n)), np.broadcast_to(st[None, :], (size, n))])
    return [jnp.asarray(np.stack(parts)), jnp.asarray(perm.astype(BF16)), jnp.asarray(rows), jnp.asarray(cols)]


def split(x):
    hi = x.astype(BF16)
    return hi, (x - hi.astype(F32)).astype(BF16)


def dot(a, b):
    return jnp.dot(a, b, preferred_element_type=F32)


def left_dot(wh, wl, x):
    xh, xl = split(x)
    return dot(wl, xh) + dot(wh, xl) + dot(wh, xh)


def right_dot(x, wh, wl):
    xh, xl = split(x)
    return dot(xh, wl) + dot(xl, wh) + dot(xh, wh)


def cat(parts, axis):
    return jnp.concatenate(parts, axis=axis)


def load_window(ext, channel, top, left, size):
    row = pl.multiple_of((top // ROWS) * ROWS, ROWS)
    base = pl.multiple_of((left // LANES) * LANES, LANES)
    width, height = size + LANES, size + ROWS
    wide = ext[channel, pl.ds(row, height), pl.ds(base, width)]
    wide = pltpu.roll(wide, (width - (left - base)) % width, 1)[:, :size]
    return pltpu.roll(wide, (height - (top - row)) % height, 0)[:size]


def add_window(acc, channel, top, left, value):
    size = value.shape[0]
    row = pl.multiple_of((top // ROWS) * ROWS, ROWS)
    base = pl.multiple_of((left // LANES) * LANES, LANES)
    width, height = size + LANES, size + ROWS
    wide = cat([value, jnp.zeros((ROWS, size), F32)], 0)
    wide = pltpu.roll(wide, top - row, 0)
    wide = cat([wide, jnp.zeros((height, LANES), F32)], 1)
    wide = pltpu.roll(wide, left - base, 1)
    acc[channel, pl.ds(row, height), pl.ds(base, width)] += wide


def clear_beyond(grid, tile, half, frame):
    end = half + tile
    strips = (
        ("up", slice(0, half), slice(None)),
        ("down", slice(end, None), slice(None)),
        ("left", slice(half, end), slice(0, half)),
        ("right", slice(half, end), slice(end, None)),
    )
    for side, rows, cols in strips:

        @pl.when(jnp.logical_not(grid.has[side]))
        def _():
            frame[:, rows, cols] = jnp.zeros_like(frame[:, rows, cols])

    for up, rows in (("up", slice(0, half)), ("down", slice(end, None))):
        for side, cols in (("left", slice(0, half)), ("right", slice(end, None))):

            @pl.when(grid.has[up] & jnp.logical_not(grid.has[side]))
            def _():
                frame[:, rows, cols] = jnp.zeros_like(frame[:, rows, cols])


class Grid:
    def __init__(self, send, recv):
        row, col = lax.axis_index("row"), lax.axis_index("col")
        self.has = {
            "up": row > 0,
            "down": row < lax.axis_size("row") - 1,
            "left": col > 0,
            "right": col < lax.axis_size("col") - 1,
        }
        self.peer = {"up": {"row": row - 1}, "down": {"row": row + 1}, "left": {"col": col - 1}, "right": {"col": col + 1}}
        self.back = {"up": "down", "down": "up", "left": "right", "right": "left"}
        self.send, self.recv = send, recv
        self.count = 0

    def greet(self):
        barrier = pltpu.get_barrier_semaphore()
        for side in self.has:

            @pl.when(self.has[side])
            def _():
                pl.semaphore_signal(barrier, inc=1, device_id=self.peer[side], device_id_type=pl.DeviceIdType.MESH)

        pl.semaphore_wait(barrier, sum(h.astype(jnp.int32) for h in self.has.values()))

    def message(self, side, src, dst, also=None):
        at = self.count
        self.count += 1
        copy = pltpu.make_async_remote_copy(
            src_ref=src,
            dst_ref=dst,
            send_sem=self.send.at[at],
            recv_sem=self.recv.at[at],
            device_id=self.peer[side],
            device_id_type=pl.DeviceIdType.MESH,
        )
        goes, comes = self.has[side], self.has[self.back[side]]
        if also is not None:
            goes, comes = goes & self.has[also], comes & self.has[also]
        return copy, goes, comes


def when(cond, act):
    if cond is True:
        act()
    else:
        pl.when(cond)(act)


def start(*messages):
    for copy, goes, _ in messages:
        pl.when(goes)(copy.start)


def arrive(*messages):
    for copy, _, comes in messages:
        pl.when(comes)(copy.wait_recv)


def leave(*messages):
    for copy, goes, _ in messages:
        pl.when(goes)(copy.wait_send)


def column_messages(grid, tile, half, src, frame):
    size, end = 2 * half, half + tile
    tops, bottoms, mids = slice(0, half), slice(tile - half, tile), slice(half, tile - half)
    ends, inner = [], []
    for rows, store, group in (
        (tops, slice(half, size), ends),
        (bottoms, slice(tile, end), ends),
        (mids, slice(size, tile), inner),
    ):
        group.append(grid.message("left", src.at[:, rows, :half], frame.at[:, store, end:]))
        group.append(grid.message("right", src.at[:, rows, tile - half :], frame.at[:, store, :half]))
    return ends, inner


def row_messages(grid, tile, half, src, frame):
    end = half + tile
    return [
        grid.message("up", src.at[:, :half, :], frame.at[:, end:, half:end]),
        grid.message("down", src.at[:, tile - half :, :], frame.at[:, :half, half:end]),
    ]


def corner_messages(grid, tile, half, frame):
    size, end = 2 * half, half + tile
    out = []
    for side, cols in (("left", slice(0, half)), ("right", slice(end, None))):
        out.append(grid.message("up", frame.at[:, half:size, cols], frame.at[:, end:, cols], also=side))
        out.append(grid.message("down", frame.at[:, tile:end, cols], frame.at[:, :half, cols], also=side))
    return out


def halo_kernel(tile, half, cells, info, frame, infos, send, recv, local):
    grid = Grid(send, recv)
    ends, inner = column_messages(grid, tile, half, cells, frame)
    rows = row_messages(grid, tile, half, cells, frame)
    corners = corner_messages(grid, tile, half, frame)
    tags = [
        grid.message("left", info.at[0], infos.at[1, 2]),
        grid.message("right", info.at[0], infos.at[1, 0]),
    ]
    bands = [
        grid.message("up", infos.at[1], infos.at[2]),
        grid.message("down", infos.at[1], infos.at[0]),
    ]
    fills = [
        (pltpu.make_async_copy(info.at[0], infos.at[1, 1], local.at[0]), True),
        (pltpu.make_async_copy(info.at[1], infos.at[1, 0], local.at[1]), jnp.logical_not(grid.has["left"])),
        (pltpu.make_async_copy(info.at[1], infos.at[1, 2], local.at[2]), jnp.logical_not(grid.has["right"])),
        (pltpu.make_async_copy(info.at[pl.ds(1, 3)], infos.at[0], local.at[3]), jnp.logical_not(grid.has["up"])),
        (pltpu.make_async_copy(info.at[pl.ds(1, 3)], infos.at[2], local.at[4]), jnp.logical_not(grid.has["down"])),
        (pltpu.make_async_copy(cells, frame.at[:, half : half + tile, half : half + tile], local.at[5]), True),
    ]
    for copy, cond in fills:
        when(cond, copy.start)
    grid.greet()
    start(*tags, *ends, *inner, *rows)
    clear_beyond(grid, tile, half, frame)
    for copy, cond in fills:
        when(cond, copy.wait)
    arrive(*tags)
    start(*bands)
    arrive(*ends)
    start(*corners)
    arrive(*inner, *rows, *bands, *corners)
    leave(*tags, *ends, *inner, *rows, *bands, *corners)


def update_kernel(tile, half, *refs):
    acc, cells, weight, frame = refs[:4]
    fa, fb, g_lm, g_rm, g_le, g_re, s_le, s_re, send, recv = refs[4:]
    size, end = 2 * half, half + tile
    grid = Grid(send, recv)
    has = grid.has
    val = frame.at[:, half:end, half:end]
    up = grid.message("up", acc.at[:, :half, :], fb)
    down = grid.message("down", acc.at[:, end:, :], fa)
    mids = [
        grid.message("left", acc.at[:, size:tile, :half], g_rm),
        grid.message("right", acc.at[:, size:tile, end:], g_lm),
    ]
    ends = [grid.message("left", s_le, g_re), grid.message("right", s_re, g_le)]
    new_ends, new_inner = column_messages(grid, tile, half, val, frame)
    new_rows = row_messages(grid, tile, half, val, frame)
    corners = corner_messages(grid, tile, half, frame)
    grid.greet()
    start(up, down, *mids)
    clear_beyond(grid, tile, half, frame)
    for side, buffers in (("up", (fa,)), ("down", (fb,)), ("left", (g_lm, g_le)), ("right", (g_rm, g_re))):

        @pl.when(jnp.logical_not(has[side]))
        def _():
            for b in buffers:
                b[...] = jnp.zeros_like(b)

    arrive(up, down)
    for ch in range(2):
        s_le[ch, 0] = acc[ch, half:size, :half] + fa[ch, :, :half]
        s_le[ch, 1] = acc[ch, tile:end, :half] + fb[ch, :, :half]
        s_re[ch, 0] = acc[ch, half:size, end:] + fa[ch, :, end:]
        s_re[ch, 1] = acc[ch, tile:end, end:] + fb[ch, :, end:]
    start(*ends)
    tops, bottoms, inner = slice(0, half), slice(tile - half, tile), slice(half, tile - half)
    heads, tails = slice(0, half), slice(tile - half, tile)

    def moved(at):
        return slice(at.start + half, at.stop + half)

    def settle(ch, rows, cols, more):
        total = acc[ch, moved(rows), moved(cols)] + BETA * cells[ch, rows, cols]
        for m in more:
            total = total + m
        frame[ch, moved(rows), moved(cols)] = total / weight[rows, cols]

    for ch in range(2):
        settle(ch, inner, inner, ())
        settle(ch, tops, inner, (fa[ch, :, size:tile],))
        settle(ch, bottoms, inner, (fb[ch, :, size:tile],))
    arrive(*mids)
    for ch in range(2):
        settle(ch, inner, heads, (g_lm[ch],))
        settle(ch, inner, tails, (g_rm[ch],))
    start(*new_inner)
    arrive(*ends)
    for ch in range(2):
        settle(ch, tops, heads, (fa[ch, :, half:size], g_le[ch, 0]))
        settle(ch, bottoms, heads, (fb[ch, :, half:size], g_le[ch, 1]))
        settle(ch, tops, tails, (fa[ch, :, tile:end], g_re[ch, 0]))
        settle(ch, bottoms, tails, (fb[ch, :, tile:end], g_re[ch, 1]))
    start(*new_ends, *new_rows)
    arrive(*new_ends)
    start(*corners)
    arrive(*new_inner, *new_rows, *corners)
    leave(up, down, *mids, *ends, *new_ends, *new_inner, *new_rows, *corners)


def add_weights(tile, half, slots, info, acc, power):
    size = 2 * half

    def body(index, carry):
        owner = index // slots
        slot = index % slots
        r, c = owner // 3, owner % 3
        top = info[r, c, 0, slot] + (r - 1) * tile + half
        left = info[r, c, 0, slots + slot] + (c - 1) * tile + half
        live = info[r, c, 0, 2 * slots]
        hit = (slot < live) & (top > 0) & (top < size + tile) & (left > 0) & (left < size + tile)

        @pl.when(hit)
        def _():
            add_window(acc, 0, top, left, power[...])

        return carry

    lax.fori_loop(0, 9 * slots, body, 0)


def project_kernel(tile, half, info, *refs):
    ext, probe, dual, amp, wt, perm, twr, twc = refs[:8]
    base, acc, weight, heavy, power, strips = refs[8:]
    slots = dual.shape[1]
    size = 2 * half
    acc[...] = jnp.zeros_like(acc)
    heavy[...] = jnp.full_like(heavy, BETA)
    power[...] = probe[0] * probe[0] + probe[1] * probe[1]
    add_weights(tile, half, slots, info, heavy, power)
    weight[...] = heavy[0, size : size + tile, size : size + tile]
    live = info[1, 1, 0, 2 * slots]

    def skip(slot, carry):
        base[:, slot] = dual[:, slot]
        return carry

    def step(slot, carry):
        top = info[1, 1, 0, slot]
        left = info[1, 1, 0, slots + slot]
        pr, pi = probe[0], probe[1]
        sr = load_window(ext, 0, top, left, size)
        si = load_window(ext, 1, top, left, size)
        re = pr * sr - pi * si + dual[0, slot]
        im = pr * si + pi * sr + dual[1, slot]
        fh, fl, ih, il = wt[0], wt[1], wt[2], wt[3]
        cr, sr_ = twr[0], twr[1]
        cc, sc = twc[0], twc[1]
        dr, di = re[:half] - re[half:], im[:half] - im[half:]
        x = cat(
            [
                cat([re[:half] + re[half:], dr * cr + di * sr_], 1),
                cat([im[:half] + im[half:], di * cr - dr * sr_], 1),
            ],
            0,
        )
        y = left_dot(fh, fl, x)
        re = cat([y[:half, :size], y[:half, size:]], 0)
        im = cat([y[half:, :size], y[half:, size:]], 0)
        dr, di = re[:, :half] - re[:, half:], im[:, :half] - im[:, half:]
        x = cat(
            [
                cat([re[:, :half] + re[:, half:], im[:, :half] + im[:, half:]], 1),
                cat([dr * cc + di * sc, di * cc - dr * sc], 1),
            ],
            0,
        )
        s = right_dot(x, ih, il)
        for c in range(size // LANES):
            strips[c] = amp[slot, :, c * LANES : (c + 1) * LANES]
        a = cat(
            [
                cat([strips[c, pl.ds(first, half, stride=2), :] for c in range(size // LANES)], 1)
                for first in range(2)
            ],
            0,
        )
        ah, al = split(a)
        a = dot(ah, perm[...]) + dot(al, perm[...])
        a = cat([a[:, :half], a[:, half:]], 0)
        sre, sim = s[:, :half], s[:, half:]
        fac = a * lax.rsqrt(jnp.maximum(sre * sre + sim * sim, FLOOR * FLOOR))
        x = cat([sre * fac, sim * fac], 1)
        z = right_dot(x, fh, fl)
        er, ei = z[:size, :half], z[:size, half:]
        orr, oi = z[size:, :half], z[size:, half:]
        tr, ti = orr * cc - oi * sc, oi * cc + orr * sc
        re = cat([er + tr, er - tr], 1)
        im = cat([ei + ti, ei - ti], 1)
        x = cat([cat([re[:half], re[half:]], 1), cat([im[:half], im[half:]], 1)], 0)
        y = left_dot(ih, il, x)
        er, ei = y[:half, :size], y[half:, :size]
        orr, oi = y[:half, size:], y[half:, size:]
        tr, ti = orr * cr - oi * sr_, oi * cr + orr * sr_
        dr = cat([er + tr, er - tr], 0) - dual[0, slot]
        di = cat([ei + ti, ei - ti], 0) - dual[1, slot]
        base[0, slot] = -dr
        base[1, slot] = -di
        add_window(acc, 0, top, left, pr * dr + pi * di)
        add_window(acc, 1, top, left, pr * di - pi * dr)
        return carry

    lax.fori_loop(live, slots, skip, 0)
    lax.fori_loop(0, live, step, 0)


def dual_kernel(tile, half, info, ext, probe, base, out, new, ready, sems):
    slots = base.shape[1]
    size = 2 * half
    keep = pltpu.make_async_copy(ext.at[:, half : half + tile, half : half + tile], new, sems.at[slots])
    keep.start()
    copies = []
    for slot in range(slots):
        copy = pltpu.make_async_copy(ready.at[slot], out.at[:, slot], sems.at[slot])
        copies.append(copy)
        active = slot < info[1, 1, 0, 2 * slots]

        @pl.when(jnp.logical_not(active))
        def _():
            ready[slot] = base[:, slot]

        @pl.when(active)
        def _():
            top = info[1, 1, 0, slot]
            left = info[1, 1, 0, slots + slot]
            pr, pi = probe[0], probe[1]
            sr = load_window(ext, 0, top, left, size)
            si = load_window(ext, 1, top, left, size)
            ready[slot, 0] = base[0, slot] + (pr * sr - pi * si)
            ready[slot, 1] = base[1, slot] + (pr * si + pi * sr)

        copy.start()
    for copy in copies:
        copy.wait()
    keep.wait()


def shards(object_field, probe, dual, amplitude, offsets, live):
    tile = object_field.shape[1]
    size = probe.shape[1]
    half = size // 2
    slots = dual.shape[3]
    wide = tile + size
    mid = tile - size
    lam = dual.reshape(2, slots, size, size)
    amps = amplitude.reshape(slots, size, size)
    sd = lambda *shape: jax.ShapeDtypeStruct(shape, F32)
    dma = lambda n: pltpu.SemaphoreType.DMA((n,))

    own = jnp.concatenate([offsets[0, 0, 0], offsets[1, 0, 0], live[0]])
    tag = jnp.pad(own[None, None], ((0, 3), (0, ROWS - 1), (0, LANES - own.shape[0])))

    frame, infos = pl.pallas_call(
        functools.partial(halo_kernel, tile, half),
        out_shape=(sd(2, wide, wide), jax.ShapeDtypeStruct((3, 3, ROWS, LANES), jnp.int32)),
        in_specs=[ANY, ANY],
        out_specs=(VM, ANY),
        scratch_shapes=[dma(16), dma(16), dma(6)],
        compiler_params=pltpu.CompilerParams(collective_id=0, has_side_effects=True, vmem_limit_bytes=2 * MIB),
        cost_estimate=pl.CostEstimate(flops=0, bytes_accessed=80_000_000, transcendentals=0),
        name="halo",
    )(object_field, tag)

    cost = lambda size: pl.CostEstimate(flops=0, bytes_accessed=size, transcendentals=0)
    base, acc, weight = pl.pallas_call(
        functools.partial(project_kernel, tile, half),
        out_shape=(sd(2, slots, size, size), sd(2, wide, wide), sd(tile, tile)),
        in_specs=[SM] + [VM] * 8,
        out_specs=(VM, VM, VM),
        scratch_shapes=[
            pltpu.VMEM((1, tile + 2 * size, tile + 2 * size), F32),
            pltpu.VMEM((size, size), F32),
            pltpu.VMEM((size // LANES, size, LANES), F32),
        ],
        compiler_params=pltpu.CompilerParams(vmem_limit_bytes=16 * MIB),
        cost_estimate=cost(30_000_000),
        name="project",
    )(infos, frame, probe, lam, amps, *tables(size))

    strip, side, end = (2, half, wide), (2, mid, half), (2, 2, half, half)
    frame = pl.pallas_call(
        functools.partial(update_kernel, tile, half),
        out_shape=sd(2, wide, wide),
        in_specs=[VM] * 3,
        out_specs=VM,
        scratch_shapes=[pltpu.VMEM(x, F32) for x in (strip, strip, side, side, end, end, end, end)] + [dma(18), dma(18)],
        compiler_params=pltpu.CompilerParams(collective_id=1, has_side_effects=True, vmem_limit_bytes=8 * MIB),
        cost_estimate=cost(150_000_000),
        name="update",
    )(acc, object_field, weight)

    dual_new, new = pl.pallas_call(
        functools.partial(dual_kernel, tile, half),
        out_shape=(sd(2, slots, size, size), sd(2, tile, tile)),
        in_specs=[SM, VM, VM, VM],
        out_specs=(ANY, ANY),
        scratch_shapes=[pltpu.VMEM((slots, 2, size, size), F32), dma(slots + 1)],
        compiler_params=pltpu.CompilerParams(vmem_limit_bytes=12 * MIB),
        name="renew",
    )(infos, frame, probe, base)
    return new, dual_new.reshape(dual.shape)


def solution(mesh):
    placed = (
        P(None, "row", "col"),
        P(),
        P(None, "row", "col", None, None, None),
        P("row", "col", None, None, None),
        P(None, "row", "col", None),
        P("row", "col"),
    )
    return jax.shard_map(
        shards,
        mesh=mesh,
        in_specs=placed,
        out_specs=(P(None, "row", "col"), P(None, "row", "col", None, None, None)),
        check_vma=False,
    )
```

```python
import functools
import math

import jax
import jax.numpy as jnp
import numpy as np
from jax import lax
from jax.experimental import pallas as pl
from jax.experimental.pallas import tpu as pltpu
from jax.sharding import PartitionSpec as P

FLOOR = 0.1
BETA = 1.0
LANES = 128
ROWS = 8
MIB = 1 << 20
F32 = jnp.float32
BF16 = jnp.bfloat16
ANY = pl.BlockSpec(memory_space=pl.ANY)
VM = pl.BlockSpec(memory_space=pltpu.VMEM)
SM = pl.BlockSpec(memory_space=pltpu.SMEM)


def tables(size):
    n = size // 2
    k = np.arange(n)
    angle = 2.0 * math.pi * ((k[:, None] * k[None, :]) % n) / n
    c, s = np.cos(angle) / math.sqrt(size), np.sin(angle) / math.sqrt(size)
    fwd = np.block([[c, s], [-s, c]])
    inv = np.block([[c, -s], [s, c]])
    parts = []
    for full in (fwd, inv):
        hi = full.astype(np.float32).astype(BF16)
        parts += [hi, (full - hi.astype(np.float64)).astype(np.float32).astype(BF16)]
    perm = np.zeros((size, size), np.float32)
    perm[2 * k, k] = 1.0
    perm[2 * k + 1, n + k] = 1.0
    tw = 2.0 * math.pi * k / size
    ct, st = np.cos(tw).astype(np.float32), np.sin(tw).astype(np.float32)
    rows = np.stack([np.broadcast_to(ct[:, None], (n, size)), np.broadcast_to(st[:, None], (n, size))])
    both = np.broadcast_to(np.concatenate([ct, st])[None, :], (n, size))
    waves = np.concatenate([rows, both[None]]).astype(np.float32)
    return [jnp.asarray(np.stack(parts + [perm.astype(BF16)])), jnp.asarray(waves)]


def split(x):
    hi = x.astype(BF16)
    return hi, (x - hi.astype(F32)).astype(BF16)


def dot(a, b):
    return jnp.dot(a, b, preferred_element_type=F32)


def left_dot(wh, wl, x):
    xh, xl = split(x)
    return dot(wl, xh) + dot(wh, xl) + dot(wh, xh)


def right_dot(x, wh, wl):
    xh, xl = split(x)
    return dot(xh, wl) + dot(xl, wh) + dot(xh, wh)


def cat(parts, axis):
    return jnp.concatenate(parts, axis=axis)


def load_window(ext, channel, top, left, size):
    row = pl.multiple_of((top // ROWS) * ROWS, ROWS)
    base = pl.multiple_of((left // LANES) * LANES, LANES)
    width, height = size + LANES, size + ROWS
    wide = ext[channel, pl.ds(row, height), pl.ds(base, width)]
    wide = pltpu.roll(wide, (width - (left - base)) % width, 1)[:, :size]
    return pltpu.roll(wide, (height - (top - row)) % height, 0)[:size]


def add_window(acc, channel, top, left, value):
    size = value.shape[0]
    row = pl.multiple_of((top // ROWS) * ROWS, ROWS)
    base = pl.multiple_of((left // LANES) * LANES, LANES)
    width, height = size + LANES, size + ROWS
    wide = cat([value, jnp.zeros((ROWS, size), F32)], 0)
    wide = pltpu.roll(wide, top - row, 0)
    wide = cat([wide, jnp.zeros((height, LANES), F32)], 1)
    wide = pltpu.roll(wide, left - base, 1)
    acc[channel, pl.ds(row, height), pl.ds(base, width)] += wide


def clear_beyond(grid, tile, half, frame):
    end = half + tile
    strips = (
        ("up", slice(0, half), slice(None)),
        ("down", slice(end, None), slice(None)),
        ("left", slice(half, end), slice(0, half)),
        ("right", slice(half, end), slice(end, None)),
    )
    for side, rows, cols in strips:

        @pl.when(jnp.logical_not(grid.has[side]))
        def _():
            frame[:, rows, cols] = jnp.zeros_like(frame[:, rows, cols])

    for up, rows in (("up", slice(0, half)), ("down", slice(end, None))):
        for side, cols in (("left", slice(0, half)), ("right", slice(end, None))):

            @pl.when(grid.has[up] & jnp.logical_not(grid.has[side]))
            def _():
                frame[:, rows, cols] = jnp.zeros_like(frame[:, rows, cols])


class Grid:
    def __init__(self, send, recv):
        row, col = lax.axis_index("row"), lax.axis_index("col")
        self.has = {
            "up": row > 0,
            "down": row < lax.axis_size("row") - 1,
            "left": col > 0,
            "right": col < lax.axis_size("col") - 1,
        }
        self.peer = {"up": {"row": row - 1}, "down": {"row": row + 1}, "left": {"col": col - 1}, "right": {"col": col + 1}}
        self.back = {"up": "down", "down": "up", "left": "right", "right": "left"}
        self.send, self.recv = send, recv
        self.count = 0

    def greet(self):
        barrier = pltpu.get_barrier_semaphore()
        for side in self.has:

            @pl.when(self.has[side])
            def _():
                pl.semaphore_signal(barrier, inc=1, device_id=self.peer[side], device_id_type=pl.DeviceIdType.MESH)

        pl.semaphore_wait(barrier, sum(h.astype(jnp.int32) for h in self.has.values()))

    def message(self, side, src, dst, also=None):
        at = self.count
        self.count += 1
        copy = pltpu.make_async_remote_copy(
            src_ref=src,
            dst_ref=dst,
            send_sem=self.send.at[at],
            recv_sem=self.recv.at[at],
            device_id=self.peer[side],
            device_id_type=pl.DeviceIdType.MESH,
        )
        goes, comes = self.has[side], self.has[self.back[side]]
        if also is not None:
            goes, comes = goes & self.has[also], comes & self.has[also]
        return copy, goes, comes


def when(cond, act):
    if cond is True:
        act()
    else:
        pl.when(cond)(act)


def start(*messages):
    for copy, goes, _ in messages:
        pl.when(goes)(copy.start)


def arrive(*messages):
    for copy, _, comes in messages:
        pl.when(comes)(copy.wait_recv)


def leave(*messages):
    for copy, goes, _ in messages:
        pl.when(goes)(copy.wait_send)


def column_messages(grid, tile, half, src, frame):
    size, end = 2 * half, half + tile
    tops, bottoms, mids = slice(0, half), slice(tile - half, tile), slice(half, tile - half)
    ends, inner = [], []
    for rows, store, group in (
        (tops, slice(half, size), ends),
        (bottoms, slice(tile, end), ends),
        (mids, slice(size, tile), inner),
    ):
        group.append(grid.message("left", src.at[:, rows, :half], frame.at[:, store, end:]))
        group.append(grid.message("right", src.at[:, rows, tile - half :], frame.at[:, store, :half]))
    return ends, inner


def row_messages(grid, tile, half, src, frame):
    end = half + tile
    return [
        grid.message("up", src.at[:, :half, :], frame.at[:, end:, half:end]),
        grid.message("down", src.at[:, tile - half :, :], frame.at[:, :half, half:end]),
    ]


def corner_messages(grid, tile, half, frame):
    size, end = 2 * half, half + tile
    out = []
    for side, cols in (("left", slice(0, half)), ("right", slice(end, None))):
        out.append(grid.message("up", frame.at[:, half:size, cols], frame.at[:, end:, cols], also=side))
        out.append(grid.message("down", frame.at[:, tile:end, cols], frame.at[:, :half, cols], also=side))
    return out


def halo_kernel(tile, half, cells, info, frame, infos, send, recv, local):
    grid = Grid(send, recv)
    ends, inner = column_messages(grid, tile, half, cells, frame)
    rows = row_messages(grid, tile, half, cells, frame)
    corners = corner_messages(grid, tile, half, frame)
    tags = [
        grid.message("left", info.at[0], infos.at[1, 2]),
        grid.message("right", info.at[0], infos.at[1, 0]),
    ]
    bands = [
        grid.message("up", infos.at[1], infos.at[2]),
        grid.message("down", infos.at[1], infos.at[0]),
    ]
    fills = [
        (pltpu.make_async_copy(info.at[0], infos.at[1, 1], local.at[0]), True),
        (pltpu.make_async_copy(info.at[1], infos.at[1, 0], local.at[1]), jnp.logical_not(grid.has["left"])),
        (pltpu.make_async_copy(info.at[1], infos.at[1, 2], local.at[2]), jnp.logical_not(grid.has["right"])),
        (pltpu.make_async_copy(info.at[pl.ds(1, 3)], infos.at[0], local.at[3]), jnp.logical_not(grid.has["up"])),
        (pltpu.make_async_copy(info.at[pl.ds(1, 3)], infos.at[2], local.at[4]), jnp.logical_not(grid.has["down"])),
        (pltpu.make_async_copy(cells, frame.at[:, half : half + tile, half : half + tile], local.at[5]), True),
    ]
    for copy, cond in fills:
        when(cond, copy.start)
    grid.greet()
    start(*tags, *ends, *inner, *rows)
    clear_beyond(grid, tile, half, frame)
    for copy, cond in fills:
        when(cond, copy.wait)
    arrive(*tags)
    start(*bands)
    arrive(*ends)
    start(*corners)
    arrive(*inner, *rows, *bands, *corners)
    leave(*tags, *ends, *inner, *rows, *bands, *corners)


def update_kernel(tile, half, *refs):
    acc, cells, weight, frame = refs[:4]
    fa, fb, g_lm, g_rm, g_le, g_re, s_le, s_re, send, recv = refs[4:]
    size, end = 2 * half, half + tile
    grid = Grid(send, recv)
    has = grid.has
    val = frame.at[:, half:end, half:end]
    up = grid.message("up", acc.at[:, :half, :], fb)
    down = grid.message("down", acc.at[:, end:, :], fa)
    mids = [
        grid.message("left", acc.at[:, size:tile, :half], g_rm),
        grid.message("right", acc.at[:, size:tile, end:], g_lm),
    ]
    ends = [grid.message("left", s_le, g_re), grid.message("right", s_re, g_le)]
    new_ends, new_inner = column_messages(grid, tile, half, val, frame)
    new_rows = row_messages(grid, tile, half, val, frame)
    corners = corner_messages(grid, tile, half, frame)
    grid.greet()
    start(up, down, *mids)
    clear_beyond(grid, tile, half, frame)
    for side, buffers in (("up", (fa,)), ("down", (fb,)), ("left", (g_lm, g_le)), ("right", (g_rm, g_re))):

        @pl.when(jnp.logical_not(has[side]))
        def _():
            for b in buffers:
                b[...] = jnp.zeros_like(b)

    arrive(up, down)
    for ch in range(2):
        s_le[ch, 0] = acc[ch, half:size, :half] + fa[ch, :, :half]
        s_le[ch, 1] = acc[ch, tile:end, :half] + fb[ch, :, :half]
        s_re[ch, 0] = acc[ch, half:size, end:] + fa[ch, :, end:]
        s_re[ch, 1] = acc[ch, tile:end, end:] + fb[ch, :, end:]
    start(*ends)
    tops, bottoms, inner = slice(0, half), slice(tile - half, tile), slice(half, tile - half)
    heads, tails = slice(0, half), slice(tile - half, tile)

    def moved(at):
        return slice(at.start + half, at.stop + half)

    def settle(ch, rows, cols, more):
        total = acc[ch, moved(rows), moved(cols)] + BETA * cells[ch, rows, cols]
        for m in more:
            total = total + m
        frame[ch, moved(rows), moved(cols)] = total / weight[rows, cols]

    for ch in range(2):
        settle(ch, inner, inner, ())
        settle(ch, tops, inner, (fa[ch, :, size:tile],))
        settle(ch, bottoms, inner, (fb[ch, :, size:tile],))
    arrive(*mids)
    for ch in range(2):
        settle(ch, inner, heads, (g_lm[ch],))
        settle(ch, inner, tails, (g_rm[ch],))
    start(*new_inner)
    arrive(*ends)
    for ch in range(2):
        settle(ch, tops, heads, (fa[ch, :, half:size], g_le[ch, 0]))
        settle(ch, bottoms, heads, (fb[ch, :, half:size], g_le[ch, 1]))
        settle(ch, tops, tails, (fa[ch, :, tile:end], g_re[ch, 0]))
        settle(ch, bottoms, tails, (fb[ch, :, tile:end], g_re[ch, 1]))
    start(*new_ends, *new_rows)
    arrive(*new_ends)
    start(*corners)
    arrive(*new_inner, *new_rows, *corners)
    leave(up, down, *mids, *ends, *new_ends, *new_inner, *new_rows, *corners)


def add_weights(tile, half, slots, info, acc, power):
    size = 2 * half

    def body(index, carry):
        owner = index // slots
        slot = index % slots
        r, c = owner // 3, owner % 3
        top = info[r, c, 0, slot] + (r - 1) * tile + half
        left = info[r, c, 0, slots + slot] + (c - 1) * tile + half
        live = info[r, c, 0, 2 * slots]
        hit = (slot < live) & (top > 0) & (top < size + tile) & (left > 0) & (left < size + tile)

        @pl.when(hit)
        def _():
            add_window(acc, 0, top, left, power[...])

        return carry

    lax.fori_loop(0, 9 * slots, body, 0)


def project_kernel(tile, half, info, *refs):
    dual, ext, probe, amp, wt, tw = refs[:6]
    base, acc, weight, heavy, power, strips = refs[6:]
    slots = dual.shape[1]
    size = 2 * half
    acc[...] = jnp.zeros_like(acc)
    heavy[...] = jnp.full_like(heavy, BETA)
    power[...] = probe[0] * probe[0] + probe[1] * probe[1]
    add_weights(tile, half, slots, info, heavy, power)
    weight[...] = heavy[0, size : size + tile, size : size + tile]
    live = info[1, 1, 0, 2 * slots]

    def skip(slot, carry):
        base[:, slot] = dual[:, slot]
        return carry

    def many(slots_at):
        tops = [info[1, 1, 0, at] for at in slots_at]
        lefts = [info[1, 1, 0, slots + at] for at in slots_at]
        fh, fl, ih, il = wt[0], wt[1], wt[2], wt[3]
        cr, sr = tw[0], tw[1]
        cc = jnp.broadcast_to(tw[2, :1, :half], (size, half))
        sc = jnp.broadcast_to(tw[2, :1, half:], (size, half))
        n = range(len(slots_at))
        x = []
        for at, top, left in zip(slots_at, tops, lefts):
            pr, pi = probe[0], probe[1]
            wr = load_window(ext, 0, top, left, size)
            wi = load_window(ext, 1, top, left, size)
            re = pr * wr - pi * wi + dual[0, at]
            im = pr * wi + pi * wr + dual[1, at]
            dr, di = re[:half] - re[half:], im[:half] - im[half:]
            x.append(
                cat(
                    [
                        cat([re[:half] + re[half:], dr * cr + di * sr], 1),
                        cat([im[:half] + im[half:], di * cr - dr * sr], 1),
                    ],
                    0,
                )
            )
        y = left_dot(fh, fl, cat(x, 1))
        y = [y[:, 2 * size * i : 2 * size * (i + 1)] for i in n]
        x = []
        for v in y:
            re = cat([v[:half, :size], v[:half, size:]], 0)
            im = cat([v[half:, :size], v[half:, size:]], 0)
            dr, di = re[:, :half] - re[:, half:], im[:, :half] - im[:, half:]
            x.append(cat([re[:, :half] + re[:, half:], im[:, :half] + im[:, half:]], 1))
            x.append(cat([dr * cc + di * sc, di * cc - dr * sc], 1))
        s = right_dot(cat(x, 0), ih, il)
        s = [s[2 * size * i : 2 * size * (i + 1)] for i in n]
        rows = []
        for i, at in enumerate(slots_at):
            for c in range(size // LANES):
                strips[i, c] = amp[at, :, c * LANES : (c + 1) * LANES]
            for first in range(2):
                rows.append(cat([strips[i, c, pl.ds(first, half, stride=2), :] for c in range(size // LANES)], 1))
        ah, al = split(cat(rows, 0))
        a = dot(ah, wt[4]) + dot(al, wt[4])
        x = []
        for i in n:
            b = a[size * i : size * (i + 1)]
            b = cat([b[:, :half], b[:, half:]], 0)
            re, im = s[i][:, :half], s[i][:, half:]
            fac = b * lax.rsqrt(jnp.maximum(re * re + im * im, FLOOR * FLOOR))
            x.append(cat([re * fac, im * fac], 1))
        z = right_dot(cat(x, 0), fh, fl)
        x = []
        for i in n:
            v = z[2 * size * i : 2 * size * (i + 1)]
            er, ei = v[:size, :half], v[:size, half:]
            our, oui = v[size:, :half], v[size:, half:]
            tr, ti = our * cc - oui * sc, oui * cc + our * sc
            re = cat([er + tr, er - tr], 1)
            im = cat([ei + ti, ei - ti], 1)
            x.append(cat([cat([re[:half], re[half:]], 1), cat([im[:half], im[half:]], 1)], 0))
        y = left_dot(ih, il, cat(x, 1))
        for i, (at, top, left) in enumerate(zip(slots_at, tops, lefts)):
            v = y[:, 2 * size * i : 2 * size * (i + 1)]
            er, ei = v[:half, :size], v[half:, :size]
            our, oui = v[:half, size:], v[half:, size:]
            tr, ti = our * cr - oui * sr, oui * cr + our * sr
            dr = cat([er + tr, er - tr], 0) - dual[0, at]
            di = cat([ei + ti, ei - ti], 0) - dual[1, at]
            base[0, at] = -dr
            base[1, at] = -di
            pr, pi = probe[0], probe[1]
            add_window(acc, 0, top, left, pr * dr + pi * di)
            add_window(acc, 1, top, left, pr * di - pi * dr)

    def pair(index, carry):
        many([2 * index, 2 * index + 1])
        return carry

    lax.fori_loop(live, slots, skip, 0)
    lax.fori_loop(0, live // 2, pair, 0)

    @pl.when(live % 2 == 1)
    def _():
        many([live - 1])


def dual_kernel(tile, half, info, ext, probe, base, out, new, ready, sems):
    slots = base.shape[1]
    size = 2 * half
    keep = pltpu.make_async_copy(ext.at[:, half : half + tile, half : half + tile], new, sems.at[slots])
    keep.start()
    copies = []
    for slot in range(slots):
        copy = pltpu.make_async_copy(ready.at[slot], out.at[:, slot], sems.at[slot])
        copies.append(copy)
        active = slot < info[1, 1, 0, 2 * slots]

        @pl.when(jnp.logical_not(active))
        def _():
            ready[slot] = base[:, slot]

        @pl.when(active)
        def _():
            top = info[1, 1, 0, slot]
            left = info[1, 1, 0, slots + slot]
            pr, pi = probe[0], probe[1]
            sr = load_window(ext, 0, top, left, size)
            si = load_window(ext, 1, top, left, size)
            ready[slot, 0] = base[0, slot] + (pr * sr - pi * si)
            ready[slot, 1] = base[1, slot] + (pr * si + pi * sr)

        copy.start()
    for copy in copies:
        copy.wait()
    keep.wait()


def shards(object_field, probe, dual, amplitude, offsets, live):
    tile = object_field.shape[1]
    size = probe.shape[1]
    half = size // 2
    slots = dual.shape[3]
    wide = tile + size
    mid = tile - size
    lam = dual.reshape(2, slots, size, size)
    amps = amplitude.reshape(slots, size, size)
    sd = lambda *shape: jax.ShapeDtypeStruct(shape, F32)
    dma = lambda n: pltpu.SemaphoreType.DMA((n,))

    own = jnp.concatenate([offsets[0, 0, 0], offsets[1, 0, 0], live[0]])
    tag = jnp.pad(own[None, None], ((0, 3), (0, ROWS - 1), (0, LANES - own.shape[0])))

    frame, infos = pl.pallas_call(
        functools.partial(halo_kernel, tile, half),
        out_shape=(sd(2, wide, wide), jax.ShapeDtypeStruct((3, 3, ROWS, LANES), jnp.int32)),
        in_specs=[ANY, ANY],
        out_specs=(VM, ANY),
        scratch_shapes=[dma(16), dma(16), dma(6)],
        compiler_params=pltpu.CompilerParams(collective_id=0, has_side_effects=True, vmem_limit_bytes=2 * MIB),
        cost_estimate=pl.CostEstimate(flops=0, bytes_accessed=80_000_000, transcendentals=0),
        name="halo",
    )(object_field, tag)

    cost = lambda size: pl.CostEstimate(flops=0, bytes_accessed=size, transcendentals=0)
    base, acc, weight = pl.pallas_call(
        functools.partial(project_kernel, tile, half),
        out_shape=(sd(2, slots, size, size), sd(2, wide, wide), sd(tile, tile)),
        in_specs=[SM] + [VM] * 6,
        out_specs=(VM, VM, VM),
        scratch_shapes=[
            pltpu.VMEM((1, tile + 2 * size, tile + 2 * size), F32),
            pltpu.VMEM((size, size), F32),
            pltpu.VMEM((2, size // LANES, size, LANES), F32),
        ],
        compiler_params=pltpu.CompilerParams(vmem_limit_bytes=20 * MIB),
        cost_estimate=cost(30_000_000),
        name="project",
    )(infos, lam, frame, probe, amps, *tables(size))

    strip, side, end = (2, half, wide), (2, mid, half), (2, 2, half, half)
    frame = pl.pallas_call(
        functools.partial(update_kernel, tile, half),
        out_shape=sd(2, wide, wide),
        in_specs=[VM] * 3,
        out_specs=VM,
        scratch_shapes=[pltpu.VMEM(x, F32) for x in (strip, strip, side, side, end, end, end, end)] + [dma(18), dma(18)],
        compiler_params=pltpu.CompilerParams(collective_id=1, has_side_effects=True, vmem_limit_bytes=8 * MIB),
        cost_estimate=cost(150_000_000),
        name="update",
    )(acc, object_field, weight)

    dual_new, new = pl.pallas_call(
        functools.partial(dual_kernel, tile, half),
        out_shape=(sd(2, slots, size, size), sd(2, tile, tile)),
        in_specs=[SM, VM, VM, VM],
        out_specs=(ANY, ANY),
        scratch_shapes=[pltpu.VMEM((slots, 2, size, size), F32), dma(slots + 1)],
        compiler_params=pltpu.CompilerParams(vmem_limit_bytes=12 * MIB),
        name="renew",
    )(infos, frame, probe, base)
    return new, dual_new.reshape(dual.shape)


def solution(mesh):
    placed = (
        P(None, "row", "col"),
        P(),
        P(None, "row", "col", None, None, None),
        P("row", "col", None, None, None),
        P(None, "row", "col", None),
        P("row", "col"),
    )
    return jax.shard_map(
        shards,
        mesh=mesh,
        in_specs=placed,
        out_specs=(P(None, "row", "col"), P(None, "row", "col", None, None, None)),
        check_vma=False,
    )
```
